32 devices in a mesh: group: 2 (over core), trow: 2 (over y), tcol: 8 (over z, x).
Axes of the slice: x: 2, y: 2, z: 4, core: 2. Of those that a mesh axis runs over, the one named last changes fastest.
Arguments:
- displacement: float32 [3, 128, 64, 256], P(None, ('group', 'trow'), 'tcol'), may hold values from -6 to 6
- velocity: float32 [3, 128, 64, 256], P(None, ('group', 'trow'), 'tcol'), may hold values from -6 to 6
- stiffness: float32 [128, 64], P(('group', 'trow'), 'tcol'), may hold values from 4 to 12
- wet_position: float32 [3, 8192], P(None, ('group', 'trow', 'tcol')), may hold values from -6 to 6
- wet_normal: float32 [3, 8192], P(None, ('group', 'trow', 'tcol')), may hold values from -6 to 6
- wet_area: float32 [8192], P(('group', 'trow', 'tcol')), may hold values from 0.022097087 to 0.22097087
- wet_map: int32 [8192], P(('group', 'trow', 'tcol')), may hold values from 0 to 255
Outputs:
- displacement_out: float32 [3, 128, 64, 256], P(None, ('group', 'trow'), 'tcol')
- velocity_out: float32 [3, 128, 64, 256], P(None, ('group', 'trow'), 'tcol')
The draws below stay inside these ranges and needn't reach their ends.
Inputs may be any that keep to these rules, and one draw needn't show every extreme that they name: Each wet point lies on the patch of nodes of the device that holds it: wet_map gives a * 8 + b for the node (a, b) of that patch.
All inputs are finite; a program needn't handle non-finite values.
Results may differ from the reference program's by a relative error of at most 0.0018.
Values may be sent and summed in bfloat16 or wider, within the bound.
A program may use at most 128 MiB of HBM per device.

```python
import math
import jax
import jax.numpy as jnp
from jax import lax

LOADS = 64
LAYERS = 4
SUBSTEPS = 4
COUPLED = 2
WET_DEV = 256
PA = 32
PB = 8
NA = 128
NB = 64
W = 8192
N_TCOL = 8


def state_field(key, salt):
    key = jax.random.fold_in(key, salt)
    first_key = jax.random.fold_in(key, 0)
    shape = (3, NA, NB, LAYERS * LOADS)
    layer = lax.broadcasted_iota(jnp.int32, shape, 3) // LOADS
    inner = layer < LAYERS - 1
    base = jax.random.normal(first_key, shape, jnp.float32)
    values = base * jnp.where(inner, 2.5, 1.0).astype(jnp.float32)
    return jnp.clip(values, -6.0, 6.0).astype(jnp.float32)


def draw_displacement(key, part):
    return state_field(key, 7001)


def draw_velocity(key, part):
    return state_field(key, 7002)


def place_ends(result, rng, low, largest):
    shape = result.shape
    place = [jax.random.randint(jax.random.fold_in(rng, axis), (), 0, shape[axis]) for axis in range(len(shape))]
    result = result.at[tuple(place)].set(low)
    longest = shape.index(max(shape))
    place[longest] = (place[longest] + 1) % shape[longest]
    return result.at[tuple(place)].set(largest)


def levels(rng, extent, cuts, smallest, top_value):
    level, own = 1.0, jax.random.fold_in(rng, 6)
    for dim, blocks in cuts:
        draws = jnp.exp(jax.random.uniform(jax.random.fold_in(own, dim), (blocks,), jnp.float32, smallest / len(cuts), top_value / len(cuts)))
        level = level * jnp.repeat(draws, extent[dim] // blocks).reshape([-1 if axis == dim else 1 for axis in range(len(extent))])
    return level


def bell_draw(key, shape, deviation, reach, pieces=(), held_as=jnp.bfloat16):
    loudness = levels(key, shape, pieces, -0.22, 0.18) if pieces else 1.0
    values = jax.random.normal(key, shape, jnp.float32) * deviation * loudness
    return jnp.minimum(jnp.maximum(values, -reach), reach).astype(held_as)


def setup_inputs(seed: int = 0) -> dict:
    keys = jax.random.split(jax.random.key(seed), 8)
    displacement = draw_displacement(jax.random.fold_in(keys[7], 71), 0)
    velocity = draw_velocity(jax.random.fold_in(keys[7], 71), 0)
    stiffness = jnp.clip(jnp.exp(math.log(12.0) - 1.0986123 * jax.random.uniform(keys[2], (NA, NB), jnp.float32) ** levels(keys[2], (NA, NB), ((0, 4), (1, 8)), -0.2, 0.2)), 4.0, 12.0)
    wet_position = bell_draw(keys[3], (3, W), 1.0, 6.0, ((1, 32),), jnp.float32)
    wet_normal = bell_draw(keys[4], (3, W), 1.0, 6.0, ((1, 32),), jnp.float32)
    wet_area = jnp.clip(jnp.exp(math.log(0.22097087) - 2.3025851 * jax.random.uniform(keys[5], (W,), jnp.float32) ** levels(keys[5], (W,), ((0, 32),), -0.2, 0.2)), 0.022097087, 0.22097087)
    wet_map = place_ends(jax.random.randint(keys[6], (W,), 0, PA * PB), jax.random.fold_in(keys[6], 1), 0, (PA * PB) - 1).astype(jnp.int32)
    return dict(displacement=displacement, velocity=velocity, stiffness=stiffness, wet_position=wet_position, wet_normal=wet_normal, wet_area=wet_area, wet_map=wet_map)


SPHERE_AREA = 4.0 * math.pi
SMOOTHING = 0.1
TIME_STEP = 0.3
THICKNESS = 0.5
SPLINE_TAPS = (2.0 / 3.0, -1.0 / 12.0, -1.0 / 12.0, -1.0 / 6.0)

def spline_apply(padded, height, breadth, margin):
    middle = padded[:, margin:margin + height, margin:margin + breadth]
    summed = 2.0 * SPLINE_TAPS[0] * middle
    for offset in (1, 2, 3):
        along_rows = padded[:, margin + offset:margin + offset + height, margin:margin + breadth] + padded[:, margin - offset:margin - offset + height, margin:margin + breadth]
        along_cols = padded[:, margin:margin + height, margin + offset:margin + offset + breadth] + padded[:, margin:margin + height, margin - offset:margin - offset + breadth]
        summed = summed + SPLINE_TAPS[offset] * (along_rows + along_cols)
    return summed

def thickness_term(values, stride):
    above_layer = jnp.concatenate([values[..., stride:], values[..., -stride:]], axis=3)
    below_layer = jnp.concatenate([values[..., :stride], values[..., :-stride]], axis=3)
    return 2.0 * values - above_layer - below_layer

def advance(displacement, velocity, stiffness_grid, loading, in_plane):
    acceleration = -(stiffness_grid * in_plane) - THICKNESS * thickness_term(displacement, LOADS)
    outermost = acceleration[..., -LOADS:] + loading
    acceleration = jnp.concatenate([acceleration[..., :-LOADS], outermost], axis=3)
    velocity = velocity + TIME_STEP * acceleration
    displacement = displacement + TIME_STEP * velocity
    return (displacement, velocity)

def kernel_tile(position, normal, area, targets):
    delta_x = targets[0][None, :] - position[0][:, None]
    delta_y = targets[1][None, :] - position[1][:, None]
    delta_z = targets[2][None, :] - position[2][:, None]
    numerator = normal[0][:, None] * delta_x + normal[1][:, None] * delta_y + normal[2][:, None] * delta_z
    squared = delta_x * delta_x + delta_y * delta_y + delta_z * delta_z + SMOOTHING * SMOOTHING
    weighted = area[:, None] * numerator
    return (weighted / (SPHERE_AREA * squared * jnp.sqrt(squared))).astype(jnp.bfloat16)

def reference(displacement, velocity, stiffness, wet_position, wet_normal, wet_area, wet_map):
    wet_index = jnp.arange(W, dtype=jnp.int32)
    device = wet_index // WET_DEV
    node_row = device // N_TCOL * PA + wet_map // PB
    node_col = device % N_TCOL * PB + wet_map % PB
    node = (node_row * NB + node_col).astype(jnp.int32)
    block_size = math.gcd(W, 512)
    block_count = W // block_size
    target_blocks = wet_position.reshape(3, block_count, block_size).transpose(1, 0, 2)
    stiffness_grid = stiffness[None, :, :, None]
    for repeat in range(COUPLED):
        outer_layer = velocity[..., -LOADS:].reshape(3, NA * NB, LOADS)
        picked = jnp.take(outer_layer, node, axis=1)
        speeds = (wet_normal[0][:, None] * picked[0] + wet_normal[1][:, None] * picked[1] + wet_normal[2][:, None] * picked[2]).T
        speed_rounded = lax.optimization_barrier(speeds.astype(jnp.bfloat16)).astype(jnp.float32)

        def block_product(targets):
            tile = lax.optimization_barrier(kernel_tile(wet_position, wet_normal, wet_area, targets)).astype(jnp.float32)
            return jnp.dot(speed_rounded, tile, precision=lax.Precision.HIGHEST)
        products = lax.map(block_product, target_blocks)
        summed = products.transpose(1, 0, 2).reshape(LOADS, W)
        pressure = 0.5 * speeds + summed
        contribution = -(wet_normal[:, :, None] * pressure.T[None, :, :])
        loading = jnp.stack([jax.ops.segment_sum(contribution[component], node, num_segments=NA * NB) for component in range(3)])
        loading = loading.reshape(3, NA, NB, LOADS)

        def evolve(state):
            position_now, speed_now, force_now = state
            for substep in range(SUBSTEPS):
                padded = jnp.pad(position_now, ((0, 0), (3, 3), (3, 3), (0, 0)))
                in_plane = spline_apply(padded, NA, NB, 3)
                position_now, speed_now = advance(position_now, speed_now, stiffness_grid, force_now, in_plane)
            return (position_now, speed_now)
        displacement, velocity = lax.map(evolve, (displacement[:, None], velocity[:, None], loading[:, None]))
        displacement = displacement[:, 0]
        velocity = velocity[:, 0]
    return (displacement, velocity)
```

```python
import functools
import math

import jax
import jax.numpy as jnp
from jax import lax
from jax.experimental import pallas as pl
from jax.experimental.pallas import tpu as pltpu
from jax.sharding import PartitionSpec as P

LOADS = 64
SUBSTEPS = 4
COUPLED = 2

SPHERE_AREA = 4.0 * math.pi
SMOOTHING = 0.1
TIME_STEP = 0.3
THICKNESS = 0.5
SPLINE_TAPS = (2.0 / 3.0, -1.0 / 12.0, -1.0 / 12.0, -1.0 / 6.0)
REACH = 3
PAD = 8
MESH = pl.DeviceIdType.MESH
VMEM = pltpu.VMEM


def row_device(index, trow_count):
    return {"group": index // trow_count, "trow": lax.rem(index, trow_count)}


def whole_spec():
    return pl.BlockSpec(memory_space=pltpu.VMEM)


def gather_kernel(shape, with_geometry, *refs):
    col_count, row_count, trow_count = shape
    if with_geometry:
        (geometry, speeds, all_speeds, sources, targets, send, recv) = refs
        col_pairs = ((speeds, all_speeds), (geometry, sources))
    else:
        (speeds, all_speeds, send, recv) = refs
        col_pairs = ((speeds, all_speeds),)
    col = lax.axis_index("tcol")
    row = lax.axis_index("group") * trow_count + lax.axis_index("trow")
    barrier = pltpu.get_barrier_semaphore()

    @pl.loop(1, col_count)
    def _(d):
        pl.semaphore_signal(
            barrier, inc=1, device_id={"tcol": lax.rem(col + d, col_count)}, device_id_type=MESH
        )

    peers = col_count - 1
    if with_geometry:

        @pl.loop(1, row_count)
        def _(d):
            peer = lax.rem(row + d, row_count)
            pl.semaphore_signal(
                barrier, inc=1, device_id=row_device(peer, trow_count), device_id_type=MESH
            )

        peers = peers + row_count - 1
    pl.semaphore_wait(barrier, peers)

    def col_copy(which, d):
        source, destination = col_pairs[which]
        return pltpu.make_async_remote_copy(
            src_ref=source,
            dst_ref=destination.at[col],
            send_sem=send.at[which, d],
            recv_sem=recv.at[which, d],
            device_id={"tcol": lax.rem(col + d, col_count)},
            device_id_type=MESH,
        )

    def row_copy(d):
        return pltpu.make_async_remote_copy(
            src_ref=geometry,
            dst_ref=targets.at[row],
            send_sem=send.at[2, d],
            recv_sem=recv.at[2, d],
            device_id=row_device(lax.rem(row + d, row_count), trow_count),
            device_id_type=MESH,
        )

    if with_geometry:

        @pl.loop(1, row_count)
        def _(d):
            row_copy(d).start()

    for which in reversed(range(len(col_pairs))):

        @pl.loop(1, col_count)
        def _(d):
            col_copy(which, d).start()

        source, destination = col_pairs[which]
        destination[col] = source[...]
    if with_geometry:
        targets[row] = geometry[...]

        @pl.loop(1, row_count)
        def _(d):
            row_copy(d).wait()

    for which in range(len(col_pairs)):

        @pl.loop(1, col_count)
        def _(d):
            col_copy(which, d).wait()


def gather(shape, geometry, speeds, collective_id):
    col_count, row_count, _ = shape
    with_geometry = geometry is not None
    out_shape = [jax.ShapeDtypeStruct((col_count,) + speeds.shape, speeds.dtype)]
    if with_geometry:
        out_shape.append(jax.ShapeDtypeStruct((col_count,) + geometry.shape, geometry.dtype))
        out_shape.append(jax.ShapeDtypeStruct((row_count,) + geometry.shape, geometry.dtype))
    operands = (geometry, speeds) if with_geometry else (speeds,)
    slots = max(col_count, row_count)
    return pl.pallas_call(
        functools.partial(gather_kernel, shape, with_geometry),
        out_shape=out_shape,
        in_specs=[whole_spec()] * len(operands),
        out_specs=[whole_spec()] * len(out_shape),
        scratch_shapes=[
            pltpu.SemaphoreType.DMA((3, slots)),
            pltpu.SemaphoreType.DMA((3, slots)),
        ],
        compiler_params=pltpu.CompilerParams(
            collective_id=collective_id, has_side_effects=True
        ),
        name="gather_geometry" if with_geometry else "gather_speeds",
    )(*operands)


def tile_kernel(source_ref, target_ref, speeds_ref, tile_ref, partial_ref):
    count, _, size = speeds_ref.shape
    tx = target_ref[0, 0:1, :]
    ty = target_ref[0, 1:2, :]
    tz = target_ref[0, 2:3, :]
    partial_ref[...] = jnp.zeros_like(partial_ref)
    chunk = 64

    @pl.loop(0, count)
    def _(block):
        @pl.loop(0, size // chunk)
        def _(part):
            start = pl.multiple_of(block * size + part * chunk, chunk)
            rows = pl.ds(start, chunk)
            dx = tx - source_ref[rows, 0:1]
            dy = ty - source_ref[rows, 1:2]
            dz = tz - source_ref[rows, 2:3]
            numerator = (
                source_ref[rows, 3:4] * dx + source_ref[rows, 4:5] * dy + source_ref[rows, 5:6] * dz
            )
            squared = dx * dx + dy * dy + dz * dz + SMOOTHING * SMOOTHING
            inverse = lax.rsqrt(squared)
            value = numerator * inverse * (inverse * inverse)
            tile_ref[0, rows, :] = value.astype(jnp.bfloat16)

        rows = pl.ds(pl.multiple_of(block * size, size), size)
        partial_ref[0] += jnp.dot(
            speeds_ref[block], tile_ref[0, rows, :], preferred_element_type=jnp.float32
        )


def product_kernel(speeds_ref, tile_ref, partial_ref):
    count, _, size = speeds_ref.shape
    partial_ref[...] = jnp.zeros_like(partial_ref)

    @pl.loop(0, count)
    def _(block):
        rows = pl.ds(pl.multiple_of(block * size, size), size)
        partial_ref[0] += jnp.dot(
            speeds_ref[block], tile_ref[0, rows, :], preferred_element_type=jnp.float32
        )


def fixed(shape):
    return pl.BlockSpec(shape, lambda r: (0,) * len(shape))


def sliced(shape):
    return pl.BlockSpec((1,) + shape[1:], lambda r: (r, 0, 0))


def tile_and_product(sources, targets, speeds):
    row_count, _, size = targets.shape
    loads = speeds.shape[1]
    tile_shape = (row_count, sources.shape[0], size)
    partial_shape = (row_count, loads, size)
    return pl.pallas_call(
        tile_kernel,
        grid=(row_count,),
        out_shape=(
            jax.ShapeDtypeStruct(tile_shape, jnp.bfloat16),
            jax.ShapeDtypeStruct(partial_shape, jnp.float32),
        ),
        in_specs=[fixed(sources.shape), sliced(targets.shape), fixed(speeds.shape)],
        out_specs=(sliced(tile_shape), sliced(partial_shape)),
        name="tile_and_product",
    )(sources, targets, speeds)


def product(tiles, speeds):
    row_count, _, size = tiles.shape
    partial_shape = (row_count, speeds.shape[1], size)
    return pl.pallas_call(
        product_kernel,
        grid=(row_count,),
        out_shape=jax.ShapeDtypeStruct(partial_shape, jnp.float32),
        in_specs=[fixed(speeds.shape), sliced(tiles.shape)],
        out_specs=sliced(partial_shape),
        name="product",
    )(speeds, tiles)


def reduce_kernel(shape, partial_ref, out_ref, held, send, recv):
    _, row_count, trow_count = shape
    row = lax.axis_index("group") * trow_count + lax.axis_index("trow")
    barrier = pltpu.get_barrier_semaphore()

    @pl.loop(1, row_count)
    def _(d):
        peer = lax.rem(row + d, row_count)
        pl.semaphore_signal(
            barrier, inc=1, device_id=row_device(peer, trow_count), device_id_type=MESH
        )

    pl.semaphore_wait(barrier, row_count - 1)

    def copy(d):
        peer = lax.rem(row + d, row_count)
        return pltpu.make_async_remote_copy(
            src_ref=partial_ref.at[peer],
            dst_ref=held.at[d],
            send_sem=send.at[d],
            recv_sem=recv.at[d],
            device_id=row_device(peer, trow_count),
            device_id_type=MESH,
        )

    @pl.loop(1, row_count)
    def _(d):
        copy(d).start()

    out_ref[...] = partial_ref[row]

    @pl.loop(1, row_count)
    def _(d):
        copy(d).wait()
        out_ref[...] += held[d]


def reduce_scatter(shape, partial_value, collective_id):
    row_count = shape[1]
    block = partial_value.shape[1:]
    return pl.pallas_call(
        functools.partial(reduce_kernel, shape),
        out_shape=jax.ShapeDtypeStruct(block, jnp.float32),
        in_specs=[whole_spec()],
        out_specs=whole_spec(),
        scratch_shapes=[
            VMEM((row_count,) + block, jnp.float32),
            pltpu.SemaphoreType.DMA((row_count,)),
            pltpu.SemaphoreType.DMA((row_count,)),
        ],
        compiler_params=pltpu.CompilerParams(
            collective_id=collective_id, has_side_effects=True
        ),
        name="reduce_scatter",
    )(partial_value)


def substeps_kernel(
    shape, u_in, v_in, stiff_ref, load_ref, u_out, v_out, field, work,
    col_out, col_in, row_out, row_in, send, recv
):
    col_count, row_count, trow_count = shape
    parts, breadth, height, width = u_in.shape
    half = width // 2
    col = lax.axis_index("tcol")
    row = lax.axis_index("group") * trow_count + lax.axis_index("trow")
    present = (col > 0, col < col_count - 1, row > 0, row < row_count - 1)
    peers = (
        {"tcol": jnp.maximum(col - 1, 0)},
        {"tcol": jnp.minimum(col + 1, col_count - 1)},
        row_device(jnp.maximum(row - 1, 0), trow_count),
        row_device(jnp.minimum(row + 1, row_count - 1), trow_count),
    )
    barrier = pltpu.get_barrier_semaphore()
    for side in range(4):

        @pl.when(present[side])
        def _():
            pl.semaphore_signal(barrier, inc=1, device_id=peers[side], device_id_type=MESH)

    field[...] = jnp.zeros_like(field)
    middle = pl.ds(PAD, height)
    for part in range(parts):
        field[part, REACH : REACH + breadth, middle, :] = u_in[part]
    v_out[...] = v_in[...]
    for side in range(2):

        @pl.when(jnp.logical_not(present[side]))
        def _():
            col_in[:, side] = jnp.zeros(
                (col_in.shape[0],) + col_in.shape[2:], col_in.dtype
            )

    pl.semaphore_wait(barrier, sum(here.astype(jnp.int32) for here in present))

    def copy(step, side):
        out_buffer, in_buffer = (col_out, col_in) if side < 2 else (row_out, row_in)
        own, other = side % 2, 1 - side % 2
        return pltpu.make_async_remote_copy(
            src_ref=out_buffer.at[step, own],
            dst_ref=in_buffer.at[step, other],
            send_sem=send.at[step, side],
            recv_sem=recv.at[step, (side // 2) * 2 + other],
            device_id=peers[side],
            device_id_type=MESH,
        )

    def arrival(step, side):
        out_buffer, in_buffer = (col_out, col_in) if side < 2 else (row_out, row_in)
        return pltpu.make_async_remote_copy(
            src_ref=out_buffer.at[step, side % 2],
            dst_ref=in_buffer.at[step, side % 2],
            send_sem=send.at[step, side],
            recv_sem=recv.at[step, side],
            device_id=peers[side],
            device_id_type=MESH,
        )

    lane = lax.broadcasted_iota(jnp.int32, (height, half), 1)
    low = lane < half // 2

    @pl.loop(0, SUBSTEPS)
    def _(step):
        for side, first in ((0, REACH), (1, breadth)):

            @pl.when(present[side])
            def _():
                for part in range(parts):
                    for j in range(REACH):
                        col_out[step, side, part, j] = field[part, first + j, middle, :].astype(
                            col_out.dtype
                        )
                copy(step, side).start()

        for side, first in ((2, PAD), (3, PAD + height - REACH)):

            @pl.when(present[side])
            def _():
                for part in range(parts):
                    for j in range(breadth):
                        row_out[
                            step, side - 2, part, j // 2, (j % 2) * 4 : (j % 2) * 4 + REACH, :
                        ] = field[part, REACH + j, first : first + REACH, :]
                copy(step, side).start()

        def local(index, carry):
            part = index // breadth
            column = lax.rem(index, breadth)
            a = field[part, REACH + column, middle, 0:half]
            b = field[part, REACH + column, middle, half:width]
            turned_a = pltpu.roll(a, half // 2, 1)
            turned_b = pltpu.roll(b, half // 2, 1)
            between = jnp.where(low, turned_a, turned_b)
            edge_a = jnp.where(low, a, turned_a)
            edge_b = jnp.where(low, turned_b, b)
            stiff = stiff_ref[column]
            for lanes, here, edge in ((0, a, edge_a), (1, b, edge_b)):
                cut = pl.ds(lanes * half, half)
                summed = (2.0 * SPLINE_TAPS[0]) * here
                for offset in range(1, REACH + 1):
                    summed = summed + SPLINE_TAPS[offset] * (
                        field[part, REACH + column + offset, middle, cut]
                        + field[part, REACH + column - offset, middle, cut]
                    )
                value = -(stiff * summed) - THICKNESS * (2.0 * here - between - edge)
                if lanes == 1:
                    value = value + load_ref[part, column]
                work[part, column, :, cut] = v_out[part, column, :, cut] + TIME_STEP * value
            return carry

        lax.fori_loop(0, parts * breadth, local, 0)

        for side, first in ((2, PAD - REACH), (3, PAD + height)):

            @pl.when(present[side])
            def _():
                arrival(step, side).wait_recv()
                for part in range(parts):
                    for j in range(breadth):
                        field[part, REACH + j, first : first + REACH, :] = row_in[
                            step, side - 2, part, j // 2, (j % 2) * 4 : (j % 2) * 4 + REACH, :
                        ]

        def along_rows(index, carry):
            part = index // breadth
            column = lax.rem(index, breadth)
            stiff = stiff_ref[column] * (-TIME_STEP)
            for lanes in range(2):
                cut = pl.ds(lanes * half, half)
                summed = 0.0
                for offset in range(1, REACH + 1):
                    summed = summed + SPLINE_TAPS[offset] * (
                        field[part, REACH + column, pl.ds(PAD + offset, height), cut]
                        + field[part, REACH + column, pl.ds(PAD - offset, height), cut]
                    )
                work[part, column, :, cut] += stiff * summed
            return carry

        lax.fori_loop(0, parts * breadth, along_rows, 0)

        for side in range(2):

            @pl.when(present[side])
            def _():
                arrival(step, side).wait_recv()

        def finish(part, carry):
            for column in range(breadth):
                stiff = stiff_ref[column] * (-TIME_STEP)
                for lanes in range(2):
                    cut = pl.ds(lanes * half, half)
                    value = work[part, column, :, cut]
                    summed = None
                    for offset in range(1, REACH + 1):
                        for side, j in ((0, column - offset + REACH), (1, column + offset - breadth)):
                            inside = (column - offset < 0) if side == 0 else (column + offset >= breadth)
                            if inside:
                                term = SPLINE_TAPS[offset] * col_in[
                                    step, side, part, j, :, cut
                                ].astype(jnp.float32)
                                summed = term if summed is None else summed + term
                    if summed is not None:
                        value = value + stiff * summed
                    v_out[part, column, :, cut] = value
                    field[part, REACH + column, middle, cut] += TIME_STEP * value
            return carry

        lax.fori_loop(0, parts, finish, 0)

    for part in range(parts):
        u_out[part] = field[part, REACH : REACH + breadth, middle, :]

    @pl.loop(0, SUBSTEPS)
    def _(step):
        for side in range(4):

            @pl.when(present[side])
            def _():
                copy(step, side).wait_send()


def substeps(shape, displacement, velocity, stiff, loading, collective_id):
    parts, breadth, height, width = displacement.shape
    state = jax.ShapeDtypeStruct(displacement.shape, jnp.float32)
    cols = (SUBSTEPS, 2, parts, REACH, height, width)
    rows = (SUBSTEPS, 2, parts, breadth // 2, 8, width)
    return pl.pallas_call(
        functools.partial(substeps_kernel, shape),
        out_shape=(state, state),
        in_specs=[whole_spec()] * 4,
        out_specs=(whole_spec(), whole_spec()),
        scratch_shapes=[
            VMEM((parts, breadth + 2 * REACH, height + 2 * PAD, width), jnp.float32),
            VMEM((parts, breadth, height, width), jnp.float32),
            VMEM(cols, jnp.bfloat16),
            VMEM(cols, jnp.bfloat16),
            VMEM(rows, jnp.float32),
            VMEM(rows, jnp.float32),
            pltpu.SemaphoreType.DMA((SUBSTEPS, 4)),
            pltpu.SemaphoreType.DMA((SUBSTEPS, 4)),
        ],
        compiler_params=pltpu.CompilerParams(
            collective_id=collective_id, has_side_effects=True
        ),
        name="substeps",
    )(displacement, velocity, stiff, loading)


def normal_speeds(velocity, wet_normal, node):
    parts, breadth, height, width = velocity.shape
    flattened = velocity[..., -LOADS:].reshape(parts, breadth * height, LOADS)
    picked = jnp.take(flattened, node, axis=1)
    speeds = (
        wet_normal[0][:, None] * picked[0]
        + wet_normal[1][:, None] * picked[1]
        + wet_normal[2][:, None] * picked[2]
    )
    return speeds.T


def node_loads(pressure, wet_normal, node, breadth, height):
    count = height * breadth
    one_hot = (
        lax.broadcasted_iota(jnp.int32, (count, node.shape[0]), 0) == node[None, :]
    ).astype(jnp.float32)
    contribution = -(wet_normal[:, None, :] * pressure[None, :, :])
    loading = jnp.einsum("pw,kqw->kpq", one_hot, contribution, precision=lax.Precision.HIGHEST)
    loading = loading.reshape(3, breadth, height, LOADS)
    return jnp.pad(loading, ((0, 0), (0, 0), (0, 0), (LOADS, 0)))


def on_device(shape, displacement, velocity, stiffness, wet_position, wet_normal, wet_area, wet_map):
    height, breadth = displacement.shape[1:3]
    displacement = displacement.transpose(0, 2, 1, 3)
    velocity = velocity.transpose(0, 2, 1, 3)
    stiff = jnp.broadcast_to(stiffness.T[:, :, None], (breadth, height, 2 * LOADS))
    node = (wet_map % breadth) * height + wet_map // breadth
    scaled = wet_normal * (wet_area * (1.0 / SPHERE_AREA))[None, :]
    geometry = jnp.concatenate(
        [wet_position, scaled, jnp.zeros((2, wet_position.shape[1]), jnp.float32)], axis=0
    )
    tiles = None
    for repeat in range(COUPLED):
        speeds = normal_speeds(velocity, wet_normal, node)
        rounded = speeds.astype(jnp.bfloat16)
        if repeat == 0:
            gathered, sources, targets = gather(shape, geometry, rounded, 0)
            sources = sources.transpose(0, 2, 1).reshape(-1, geometry.shape[0])
            tiles, partial_value = tile_and_product(sources, targets, gathered)
        else:
            (gathered,) = gather(shape, None, rounded, 1)
            partial_value = product(tiles, gathered)
        received = reduce_scatter(shape, partial_value, 2)
        pressure = 0.5 * speeds + received
        loading = node_loads(pressure, wet_normal, node, breadth, height)
        displacement, velocity = substeps(shape, displacement, velocity, stiff, loading, 3)
    return (displacement.transpose(0, 2, 1, 3), velocity.transpose(0, 2, 1, 3))


def solution(mesh):
    sizes = mesh.shape
    shape = (sizes["tcol"], sizes["group"] * sizes["trow"], sizes["trow"])
    state = P(None, ("group", "trow"), "tcol", None)
    wet = ("group", "trow", "tcol")
    return jax.shard_map(
        functools.partial(on_device, shape),
        mesh=mesh,
        in_specs=(
            state,
            state,
            P(("group", "trow"), "tcol"),
            P(None, wet),
            P(None, wet),
            P(wet),
            P(wet),
        ),
        out_specs=(state, state),
        check_vma=False,
    )
```

```python
import functools
import math

import jax
import jax.numpy as jnp
from jax import lax
from jax.experimental import pallas as pl
from jax.experimental.pallas import tpu as pltpu
from jax.sharding import PartitionSpec as P

LOADS = 64
SUBSTEPS = 4
COUPLED = 2

SPHERE_AREA = 4.0 * math.pi
SMOOTHING = 0.1
TIME_STEP = 0.3
THICKNESS = 0.5
SPLINE_TAPS = (2.0 / 3.0, -1.0 / 12.0, -1.0 / 12.0, -1.0 / 6.0)
REACH = 3
PAD = 8
MESH = pl.DeviceIdType.MESH
VMEM = pltpu.VMEM


def row_device(index, trow_count):
    return {"group": index // trow_count, "trow": lax.rem(index, trow_count)}


def whole_spec():
    return pl.BlockSpec(memory_space=pltpu.VMEM)


HIGHEST = lax.Precision.HIGHEST


def coupled_kernel(
    shape, u_in, v_in, stiff_ref, position_ref, normal_ref, area_ref, node_ref, u_out, v_out,
    field, speed_now, work, load, col_out, col_in, row_out, row_in,
    geometry, sources, targets, target_cols, normal_cols, pick, spread,
    own_speeds, packed_out, packed_in, unpacked, tiles, partial_out, partial_in,
    halo_send, halo_recv, geo_send, geo_recv, speed_send, speed_recv, part_send, part_recv
):
    col_count, row_count, trow_count = shape
    parts, breadth, height, width = speed_now.shape
    half = width // 2
    points = geometry.shape[1]
    count = breadth * height
    col = lax.axis_index("tcol")
    row = lax.axis_index("group") * trow_count + lax.axis_index("trow")
    present = (col > 0, col < col_count - 1, row > 0, row < row_count - 1)
    peers = (
        {"tcol": jnp.maximum(col - 1, 0)},
        {"tcol": jnp.minimum(col + 1, col_count - 1)},
        row_device(jnp.maximum(row - 1, 0), trow_count),
        row_device(jnp.minimum(row + 1, row_count - 1), trow_count),
    )
    middle = pl.ds(PAD, height)

    def col_peer(d):
        return {"tcol": lax.rem(col + d, col_count)}

    def row_peer(d):
        return row_device(lax.rem(row + d, row_count), trow_count)

    barrier = pltpu.get_barrier_semaphore()

    @pl.loop(1, col_count)
    def _(d):
        pl.semaphore_signal(barrier, inc=1, device_id=col_peer(d), device_id_type=MESH)

    @pl.loop(1, row_count)
    def _(d):
        pl.semaphore_signal(barrier, inc=1, device_id=row_peer(d), device_id_type=MESH)

    geometry[0:3, :] = position_ref[...]
    geometry[3:6, :] = normal_ref[...] * (area_ref[...] * (1.0 / SPHERE_AREA))
    geometry[6:8, :] = jnp.zeros((2, points), jnp.float32)
    pl.semaphore_wait(barrier, col_count + row_count - 2)

    def geo_copy(kind, d):
        return pltpu.make_async_remote_copy(
            src_ref=geometry,
            dst_ref=sources.at[col] if kind == 0 else targets.at[row],
            send_sem=geo_send.at[kind, d],
            recv_sem=geo_recv.at[kind, d],
            device_id=col_peer(d) if kind == 0 else row_peer(d),
            device_id_type=MESH,
        )

    def speed_copy(repeat, d):
        return pltpu.make_async_remote_copy(
            src_ref=packed_out.at[repeat],
            dst_ref=packed_in.at[repeat, col],
            send_sem=speed_send.at[repeat, d],
            recv_sem=speed_recv.at[repeat, d],
            device_id=col_peer(d),
            device_id_type=MESH,
        )

    def part_copy(repeat, d):
        return pltpu.make_async_remote_copy(
            src_ref=partial_out.at[repeat, lax.rem(row + d, row_count)],
            dst_ref=partial_in.at[repeat, d],
            send_sem=part_send.at[repeat, d],
            recv_sem=part_recv.at[repeat, d],
            device_id=row_peer(d),
            device_id_type=MESH,
        )

    for kind, total in ((1, row_count), (0, col_count)):

        @pl.loop(1, total)
        def _(d):
            geo_copy(kind, d).start()

    sources[col] = geometry[...]
    targets[row] = geometry[...]

    field[...] = jnp.zeros_like(field)
    for part in range(parts):
        for j in range(breadth):
            for lanes in range(2):
                lines = pl.ds(lanes * breadth + j, height, stride=2 * breadth)
                cut = pl.ds(lanes * half, half)
                field[part, REACH + j, middle, cut] = u_in[part, lines, :]
                speed_now[part, j, :, cut] = v_in[part, lines, :]
    for side in range(2):

        @pl.when(jnp.logical_not(present[side]))
        def _():
            col_in[:, side] = jnp.zeros((col_in.shape[0],) + col_in.shape[2:], col_in.dtype)

    def as_column(line):
        return jnp.broadcast_to(line, (half, line.shape[1])).T

    for part in range(parts):
        normal_cols[part] = as_column(normal_ref[part : part + 1, :])
    spread[...] = (
        lax.broadcasted_iota(jnp.int32, (count, points), 0) == node_ref[...]
    ).astype(jnp.float32)
    pick[...] = spread[...].T

    def copy(step, side):
        out_buffer, in_buffer = (col_out, col_in) if side < 2 else (row_out, row_in)
        own, other = side % 2, 1 - side % 2
        return pltpu.make_async_remote_copy(
            src_ref=out_buffer.at[step, own],
            dst_ref=in_buffer.at[step, other],
            send_sem=halo_send.at[step, side],
            recv_sem=halo_recv.at[step, (side // 2) * 2 + other],
            device_id=peers[side],
            device_id_type=MESH,
        )

    def arrival(step, side):
        out_buffer, in_buffer = (col_out, col_in) if side < 2 else (row_out, row_in)
        return pltpu.make_async_remote_copy(
            src_ref=out_buffer.at[step, side % 2],
            dst_ref=in_buffer.at[step, side % 2],
            send_sem=halo_send.at[step, side],
            recv_sem=halo_recv.at[step, side],
            device_id=peers[side],
            device_id_type=MESH,
        )

    lane = lax.broadcasted_iota(jnp.int32, (height, half), 1)
    low = lane < half // 2
    low_half = lax.broadcasted_iota(jnp.int32, (points // 2, half), 1) < half // 2

    def pack(value):
        turned = pltpu.roll(value[points // 2 :], half // 2, 1)
        return jnp.where(low_half, turned, value[: points // 2])

    def tile(r):
        group = 32

        def block(index, carry):
            source = index // (points // half)
            lanes = pl.ds(pl.multiple_of(lax.rem(index, points // half) * half, half), half)
            line = [sources[source, k : k + 1, lanes] for k in range(6)]

            def rows_of(g, inner):
                rows = pl.ds(pl.multiple_of(g * group, group), group)
                dx = target_cols[r, 0, rows, :] - line[0]
                dy = target_cols[r, 1, rows, :] - line[1]
                dz = target_cols[r, 2, rows, :] - line[2]
                numerator = line[3] * dx + line[4] * dy + line[5] * dz
                squared = dx * dx + dy * dy + dz * dz + SMOOTHING * SMOOTHING
                inverse = lax.rsqrt(squared)
                value = numerator * inverse * (inverse * inverse)
                tiles[r, source, rows, lanes] = value.astype(jnp.bfloat16)
                return inner

            return lax.fori_loop(0, points // group, rows_of, carry, unroll=2)

        lax.fori_loop(0, col_count * (points // half), block, 0)

    def substep(step):
        for side, first in ((0, REACH), (1, breadth)):

            @pl.when(present[side])
            def _():
                for part in range(parts):
                    for j in range(REACH):
                        col_out[step, side, part, j] = field[part, first + j, middle, :].astype(
                            col_out.dtype
                        )
                copy(step, side).start()

        for side, first in ((2, PAD), (3, PAD + height - REACH)):

            @pl.when(present[side])
            def _():
                for part in range(parts):
                    for j in range(breadth):
                        row_out[
                            step, side - 2, part, j // 2, (j % 2) * 4 : (j % 2) * 4 + REACH, :
                        ] = field[part, REACH + j, first : first + REACH, :]
                copy(step, side).start()

        def local(index, carry):
            part = index // breadth
            column = lax.rem(index, breadth)
            a = field[part, REACH + column, middle, 0:half]
            b = field[part, REACH + column, middle, half:width]
            turned_a = pltpu.roll(a, half // 2, 1)
            turned_b = pltpu.roll(b, half // 2, 1)
            between = jnp.where(low, turned_a, turned_b)
            edge_a = jnp.where(low, a, turned_a)
            edge_b = jnp.where(low, turned_b, b)
            stiff = stiff_ref[column]
            for lanes, here, edge in ((0, a, edge_a), (1, b, edge_b)):
                cut = pl.ds(lanes * half, half)
                summed = (2.0 * SPLINE_TAPS[0]) * here
                for offset in range(1, REACH + 1):
                    summed = summed + SPLINE_TAPS[offset] * (
                        field[part, REACH + column + offset, middle, cut]
                        + field[part, REACH + column - offset, middle, cut]
                    )
                value = -(stiff * summed) - THICKNESS * (2.0 * here - between - edge)
                if lanes == 1:
                    value = value + load[part, column]
                work[part, column, :, cut] = speed_now[part, column, :, cut] + TIME_STEP * value
            return carry

        lax.fori_loop(0, parts * breadth, local, 0)

        for side, first in ((2, PAD - REACH), (3, PAD + height)):

            @pl.when(present[side])
            def _():
                arrival(step, side).wait_recv()
                for part in range(parts):
                    for j in range(breadth):
                        field[part, REACH + j, first : first + REACH, :] = row_in[
                            step, side - 2, part, j // 2, (j % 2) * 4 : (j % 2) * 4 + REACH, :
                        ]

        def along_rows(index, carry):
            part = index // breadth
            column = lax.rem(index, breadth)
            stiff = stiff_ref[column] * (-TIME_STEP)
            for lanes in range(2):
                cut = pl.ds(lanes * half, half)
                summed = 0.0
                for offset in range(1, REACH + 1):
                    summed = summed + SPLINE_TAPS[offset] * (
                        field[part, REACH + column, pl.ds(PAD + offset, height), cut]
                        + field[part, REACH + column, pl.ds(PAD - offset, height), cut]
                    )
                work[part, column, :, cut] += stiff * summed
            return carry

        lax.fori_loop(0, parts * breadth, along_rows, 0)

        for side in range(2):

            @pl.when(present[side])
            def _():
                arrival(step, side).wait_recv()

        def finish(part, carry):
            for column in range(breadth):
                stiff = stiff_ref[column] * (-TIME_STEP)
                for lanes in range(2):
                    cut = pl.ds(lanes * half, half)
                    value = work[part, column, :, cut]
                    summed = None
                    for offset in range(1, REACH + 1):
                        for side, j in ((0, column - offset + REACH), (1, column + offset - breadth)):
                            inside = (column - offset < 0) if side == 0 else (column + offset >= breadth)
                            if inside:
                                term = SPLINE_TAPS[offset] * col_in[
                                    step, side, part, j, :, cut
                                ].astype(jnp.float32)
                                summed = term if summed is None else summed + term
                    if summed is not None:
                        value = value + stiff * summed
                    speed_now[part, column, :, cut] = value
                    field[part, REACH + column, middle, cut] += TIME_STEP * value
            return carry

        lax.fori_loop(0, parts, finish, 0)

    for repeat in range(COUPLED):
        speeds = jnp.zeros((points, half), jnp.float32)
        for part in range(parts):
            outer = speed_now[part, :, :, half:width].reshape(count, half)
            picked = jnp.dot(
                pick[...], outer, precision=HIGHEST, preferred_element_type=jnp.float32
            )
            speeds = speeds + normal_cols[part] * picked
        own_speeds[...] = speeds
        packed_out[repeat] = pack(speeds).astype(packed_out.dtype)

        @pl.loop(1, col_count)
        def _(d):
            speed_copy(repeat, d).start()

        packed_in[repeat, col] = packed_out[repeat]

        if repeat == 0:

            @pl.loop(1, row_count)
            def _(d):
                geo_copy(1, d).wait_recv()

            @pl.loop(1, col_count)
            def _(d):
                geo_copy(0, d).wait_recv()

            @pl.loop(0, row_count)
            def _(r):
                for k in range(3):
                    target_cols[r, k] = as_column(targets[r, k : k + 1, :])

            tile(lax.rem(row + 1, row_count))

        @pl.loop(1, col_count)
        def _(d):
            speed_copy(repeat, d).wait_recv()

        @pl.loop(0, col_count)
        def _(c):
            value = packed_in[repeat, c].astype(jnp.float32)
            unpacked[c, 0 : points // 2, :] = value.astype(jnp.bfloat16)
            unpacked[c, points // 2 : points, :] = pltpu.roll(value, half // 2, 1).astype(
                jnp.bfloat16
            )

        @pl.loop(1, row_count + 1)
        def _(d):
            r = lax.rem(row + d, row_count)
            total = jnp.zeros((points, half), jnp.float32)
            for c in range(col_count):
                total = total + jnp.dot(
                    tiles[r, c], unpacked[c], preferred_element_type=jnp.float32
                )
            partial_out[repeat, r] = pack(total)

            @pl.when(d < row_count)
            def _():
                part_copy(repeat, d).start()
                if repeat == 0:
                    tile(lax.rem(r + 1, row_count))

        received = partial_out[repeat, row]
        for d in range(1, row_count):
            part_copy(repeat, d).wait_recv()
            received = received + partial_in[repeat, d]
        low_points = jnp.concatenate([low_half, low_half], axis=0)
        both = jnp.concatenate([received, pltpu.roll(received, half // 2, 1)], axis=0)
        pressure = jnp.where(low_points, 0.0, 0.5 * own_speeds[...] + both)
        for part in range(parts):
            loading = jnp.dot(
                spread[...], -(normal_cols[part] * pressure),
                precision=HIGHEST, preferred_element_type=jnp.float32,
            )
            load[part] = loading.reshape(breadth, height, half)

        @pl.loop(repeat * SUBSTEPS, (repeat + 1) * SUBSTEPS)
        def _(step):
            substep(step)

    for part in range(parts):
        for j in range(breadth):
            for lanes in range(2):
                lines = pl.ds(lanes * breadth + j, height, stride=2 * breadth)
                cut = pl.ds(lanes * half, half)
                u_out[part, lines, :] = field[part, REACH + j, middle, cut]
                v_out[part, lines, :] = speed_now[part, j, :, cut]

    @pl.loop(0, COUPLED * SUBSTEPS)
    def _(step):
        for side in range(4):

            @pl.when(present[side])
            def _():
                copy(step, side).wait_send()

    @pl.loop(1, col_count)
    def _(d):
        geo_copy(0, d).wait_send()
        for repeat in range(COUPLED):
            speed_copy(repeat, d).wait_send()

    @pl.loop(1, row_count)
    def _(d):
        geo_copy(1, d).wait_send()
        for repeat in range(COUPLED):
            part_copy(repeat, d).wait_send()


def on_device(shape, displacement, velocity, stiffness, wet_position, wet_normal, wet_area, wet_map):
    col_count, row_count, _ = shape
    parts, height, breadth, width = displacement.shape
    half = width // 2
    points = wet_map.shape[0]
    steps = COUPLED * SUBSTEPS
    stiff = jnp.broadcast_to(stiffness.T[:, :, None], (breadth, height, half))
    node = (wet_map % breadth) * height + wet_map // breadth

    def split(state):
        tiled = state.reshape(parts, height, breadth, 2, half).transpose(0, 1, 3, 2, 4)
        return tiled.reshape(parts, height * 2 * breadth, half)

    def joined(state):
        tiled = state.reshape(parts, height, 2, breadth, half).transpose(0, 1, 3, 2, 4)
        return tiled.reshape(parts, height, breadth, width)

    state = jax.ShapeDtypeStruct((parts, height * 2 * breadth, half), jnp.float32)
    cols = (steps, 2, parts, REACH, height, width)
    rows = (steps, 2, parts, breadth // 2, 8, width)
    f32, bf16 = jnp.float32, jnp.bfloat16
    dma = pltpu.SemaphoreType.DMA
    u_new, v_new = pl.pallas_call(
        functools.partial(coupled_kernel, shape),
        out_shape=(state, state),
        in_specs=[whole_spec()] * 7,
        out_specs=(whole_spec(), whole_spec()),
        scratch_shapes=[
            VMEM((parts, breadth + 2 * REACH, height + 2 * PAD, width), f32),
            VMEM((parts, breadth, height, width), f32),
            VMEM((parts, breadth, height, width), f32),
            VMEM((parts, breadth, height, half), f32),
            VMEM(cols, bf16),
            VMEM(cols, bf16),
            VMEM(rows, f32),
            VMEM(rows, f32),
            VMEM((8, points), f32),
            VMEM((col_count, 8, points), f32),
            VMEM((row_count, 8, points), f32),
            VMEM((row_count, 3, points, half), f32),
            VMEM((parts, points, half), f32),
            VMEM((points, height * breadth), f32),
            VMEM((height * breadth, points), f32),
            VMEM((points, half), f32),
            VMEM((COUPLED, points // 2, half), bf16),
            VMEM((COUPLED, col_count, points // 2, half), bf16),
            VMEM((col_count, points, half), bf16),
            VMEM((row_count, col_count, points, points), bf16),
            VMEM((COUPLED, row_count, points // 2, half), f32),
            VMEM((COUPLED, row_count, points // 2, half), f32),
            dma((steps, 4)),
            dma((steps, 4)),
            dma((2, max(col_count, row_count))),
            dma((2, max(col_count, row_count))),
            dma((COUPLED, col_count)),
            dma((COUPLED, col_count)),
            dma((COUPLED, row_count)),
            dma((COUPLED, row_count)),
        ],
        compiler_params=pltpu.CompilerParams(
            collective_id=0, has_side_effects=True, vmem_limit_bytes=67043328
        ),
        name="coupled_steps",
    )(
        split(displacement), split(velocity), stiff,
        wet_position, wet_normal, wet_area[None, :], node[None, :],
    )
    return (joined(u_new), joined(v_new))


def solution(mesh):
    sizes = mesh.shape
    shape = (sizes["tcol"], sizes["group"] * sizes["trow"], sizes["trow"])
    state = P(None, ("group", "trow"), "tcol", None)
    wet = ("group", "trow", "tcol")
    return jax.shard_map(
        functools.partial(on_device, shape),
        mesh=mesh,
        in_specs=(
            state,
            state,
            P(("group", "trow"), "tcol"),
            P(None, wet),
            P(None, wet),
            P(wet),
            P(wet),
        ),
        out_specs=(state, state),
        check_vma=False,
    )
```

```python
import functools
import math

import jax
import jax.numpy as jnp
from jax import lax
from jax.experimental import pallas as pl
from jax.experimental.pallas import tpu as pltpu
from jax.sharding import PartitionSpec as P

LOADS = 64
SUBSTEPS = 4
COUPLED = 2

SPHERE_AREA = 4.0 * math.pi
SMOOTHING = 0.1
TIME_STEP = 0.3
THICKNESS = 0.5
SPLINE_TAPS = (2.0 / 3.0, -1.0 / 12.0, -1.0 / 12.0, -1.0 / 6.0)
REACH = 3
PAD = 8
MESH = pl.DeviceIdType.MESH
VMEM = pltpu.VMEM


def row_device(index, trow_count):
    return {"group": index // trow_count, "trow": lax.rem(index, trow_count)}


def whole_spec():
    return pl.BlockSpec(memory_space=pltpu.VMEM)


HIGHEST = lax.Precision.HIGHEST


def coupled_kernel(
    shape, u_in, v_in, stiff_ref, position_ref, normal_ref, area_ref, node_ref, u_out, v_out,
    field, speed_now, work, load, col_out, col_in, row_out, row_in,
    geometry, sources, targets, target_cols, normal_cols, pick, spread,
    own_speeds, packed_out, packed_in, unpacked, tiles, partial_out, partial_in,
    halo_send, halo_recv, geo_send, geo_recv, speed_send, speed_recv, part_send, part_recv
):
    col_count, row_count, trow_count = shape
    parts, breadth, height, width = speed_now.shape
    half = width // 2
    points = geometry.shape[1]
    count = breadth * height
    col = lax.axis_index("tcol")
    row = lax.axis_index("group") * trow_count + lax.axis_index("trow")
    present = (col > 0, col < col_count - 1, row > 0, row < row_count - 1)
    peers = (
        {"tcol": jnp.maximum(col - 1, 0)},
        {"tcol": jnp.minimum(col + 1, col_count - 1)},
        row_device(jnp.maximum(row - 1, 0), trow_count),
        row_device(jnp.minimum(row + 1, row_count - 1), trow_count),
    )
    middle = pl.ds(PAD, height)

    def col_peer(d):
        return {"tcol": lax.rem(col + d, col_count)}

    def row_peer(d):
        return row_device(lax.rem(row + d, row_count), trow_count)

    barrier = pltpu.get_barrier_semaphore()

    @pl.loop(1, col_count)
    def _(d):
        pl.semaphore_signal(barrier, inc=1, device_id=col_peer(d), device_id_type=MESH)

    @pl.loop(1, row_count)
    def _(d):
        pl.semaphore_signal(barrier, inc=1, device_id=row_peer(d), device_id_type=MESH)

    geometry[0:3, :] = position_ref[...]
    geometry[3:6, :] = normal_ref[...] * (area_ref[...] * (1.0 / SPHERE_AREA))
    geometry[6:8, :] = jnp.zeros((2, points), jnp.float32)
    pl.semaphore_wait(barrier, col_count + row_count - 2)

    def geo_copy(kind, d):
        return pltpu.make_async_remote_copy(
            src_ref=geometry,
            dst_ref=sources.at[col] if kind == 0 else targets.at[row],
            send_sem=geo_send.at[kind, d],
            recv_sem=geo_recv.at[kind, d],
            device_id=col_peer(d) if kind == 0 else row_peer(d),
            device_id_type=MESH,
        )

    def speed_copy(repeat, d):
        return pltpu.make_async_remote_copy(
            src_ref=packed_out.at[repeat],
            dst_ref=packed_in.at[repeat, col],
            send_sem=speed_send.at[repeat, d],
            recv_sem=speed_recv.at[repeat, d],
            device_id=col_peer(d),
            device_id_type=MESH,
        )

    def part_copy(repeat, d):
        return pltpu.make_async_remote_copy(
            src_ref=partial_out.at[repeat, lax.rem(row + d, row_count)],
            dst_ref=partial_in.at[repeat, d],
            send_sem=part_send.at[repeat, d],
            recv_sem=part_recv.at[repeat, d],
            device_id=row_peer(d),
            device_id_type=MESH,
        )

    for kind, total in ((1, row_count), (0, col_count)):

        @pl.loop(1, total)
        def _(d):
            geo_copy(kind, d).start()

    sources[col] = geometry[...]
    targets[row] = geometry[...]

    field[...] = jnp.zeros_like(field)
    for part in range(parts):
        for j in range(breadth):
            for lanes in range(2):
                lines = pl.ds(lanes * breadth + j, height, stride=2 * breadth)
                cut = pl.ds(lanes * half, half)
                field[part, REACH + j, middle, cut] = u_in[part, lines, :]
                speed_now[part, j, :, cut] = v_in[part, lines, :]
    for side in range(2):

        @pl.when(jnp.logical_not(present[side]))
        def _():
            col_in[:, :, side] = jnp.zeros(col_in.shape[:2] + col_in.shape[3:], col_in.dtype)

    def as_column(line):
        return jnp.broadcast_to(line, (half, line.shape[1])).T

    for part in range(parts):
        normal_cols[part] = as_column(normal_ref[part : part + 1, :])
    spread[...] = (
        lax.broadcasted_iota(jnp.int32, (count, points), 0) == node_ref[...]
    ).astype(jnp.float32)
    pick[...] = spread[...].T

    def halo_copy(step, side, part, arriving):
        out_buffer, in_buffer = (col_out, col_in) if side < 2 else (row_out, row_in)
        own = side % 2
        other = own if arriving else 1 - own
        return pltpu.make_async_remote_copy(
            src_ref=out_buffer.at[step, part, own],
            dst_ref=in_buffer.at[step, part, other],
            send_sem=halo_send.at[step, part, side],
            recv_sem=halo_recv.at[step, part, (side // 2) * 2 + other],
            device_id=peers[side],
            device_id_type=MESH,
        )

    lane = lax.broadcasted_iota(jnp.int32, (height, half), 1)
    low = lane < half // 2
    low_half = lax.broadcasted_iota(jnp.int32, (points // 2, half), 1) < half // 2

    def pack(value):
        turned = pltpu.roll(value[points // 2 :], half // 2, 1)
        return jnp.where(low_half, turned, value[: points // 2])

    def tile(r):
        group = 32

        def block(index, carry):
            source = index // (points // half)
            lanes = pl.ds(pl.multiple_of(lax.rem(index, points // half) * half, half), half)
            line = [sources[source, k : k + 1, lanes] for k in range(6)]

            def rows_of(g, inner):
                rows = pl.ds(pl.multiple_of(g * group, group), group)
                dx = target_cols[r, 0, rows, :] - line[0]
                dy = target_cols[r, 1, rows, :] - line[1]
                dz = target_cols[r, 2, rows, :] - line[2]
                numerator = line[3] * dx + line[4] * dy + line[5] * dz
                squared = dx * dx + dy * dy + dz * dz + SMOOTHING * SMOOTHING
                inverse = lax.rsqrt(squared)
                value = numerator * inverse * (inverse * inverse)
                tiles[r, source, rows, lanes] = value.astype(jnp.bfloat16)
                return inner

            return lax.fori_loop(0, points // group, rows_of, carry, unroll=2)

        lax.fori_loop(0, col_count * (points // half), block, 0)

    def send_halos(step, part):
        for side, first in ((0, REACH), (1, breadth)):

            @pl.when(present[side])
            def _():
                for j in range(REACH):
                    col_out[step, part, side, j] = field[part, first + j, middle, :].astype(
                        col_out.dtype
                    )
                halo_copy(step, side, part, False).start()

        for side, first in ((2, PAD), (3, PAD + height - REACH)):

            @pl.when(present[side])
            def _():
                for j in range(breadth):
                    row_out[
                        step, part, side - 2, j // 2, (j % 2) * 4 : (j % 2) * 4 + REACH, :
                    ] = field[part, REACH + j, first : first + REACH, :]
                halo_copy(step, side, part, False).start()

    def local(part):
        def body(column, carry):
            a = field[part, REACH + column, middle, 0:half]
            b = field[part, REACH + column, middle, half:width]
            turned_a = pltpu.roll(a, half // 2, 1)
            turned_b = pltpu.roll(b, half // 2, 1)
            between = jnp.where(low, turned_a, turned_b)
            edge_a = jnp.where(low, a, turned_a)
            edge_b = jnp.where(low, turned_b, b)
            stiff = stiff_ref[column]
            for lanes, here, edge in ((0, a, edge_a), (1, b, edge_b)):
                cut = pl.ds(lanes * half, half)
                summed = (2.0 * SPLINE_TAPS[0]) * here
                for offset in range(1, REACH + 1):
                    summed = summed + SPLINE_TAPS[offset] * (
                        field[part, REACH + column + offset, middle, cut]
                        + field[part, REACH + column - offset, middle, cut]
                    )
                value = -(stiff * summed) - THICKNESS * (2.0 * here - between - edge)
                if lanes == 1:
                    value = value + load[part, column]
                work[part, column, :, cut] = speed_now[part, column, :, cut] + TIME_STEP * value
            return carry

        lax.fori_loop(0, breadth, body, 0)

    def complete(step, part):
        for side, first in ((2, PAD - REACH), (3, PAD + height)):

            @pl.when(present[side])
            def _():
                halo_copy(step, side, part, True).wait_recv()
                for j in range(breadth):
                    field[part, REACH + j, first : first + REACH, :] = row_in[
                        step, part, side - 2, j // 2, (j % 2) * 4 : (j % 2) * 4 + REACH, :
                    ]

        def along_rows(column, carry):
            stiff = stiff_ref[column] * (-TIME_STEP)
            for lanes in range(2):
                cut = pl.ds(lanes * half, half)
                summed = 0.0
                for offset in range(1, REACH + 1):
                    summed = summed + SPLINE_TAPS[offset] * (
                        field[part, REACH + column, pl.ds(PAD + offset, height), cut]
                        + field[part, REACH + column, pl.ds(PAD - offset, height), cut]
                    )
                work[part, column, :, cut] += stiff * summed
            return carry

        lax.fori_loop(0, breadth, along_rows, 0)

        for side in range(2):

            @pl.when(present[side])
            def _():
                halo_copy(step, side, part, True).wait_recv()

        for column in range(breadth):
            stiff = stiff_ref[column] * (-TIME_STEP)
            for lanes in range(2):
                cut = pl.ds(lanes * half, half)
                value = work[part, column, :, cut]
                summed = None
                for offset in range(1, REACH + 1):
                    for side, j in ((0, column - offset + REACH), (1, column + offset - breadth)):
                        inside = (column - offset < 0) if side == 0 else (column + offset >= breadth)
                        if inside:
                            term = SPLINE_TAPS[offset] * col_in[
                                step, part, side, j, :, cut
                            ].astype(jnp.float32)
                            summed = term if summed is None else summed + term
                if summed is not None:
                    value = value + stiff * summed
                speed_now[part, column, :, cut] = value
                field[part, REACH + column, middle, cut] += TIME_STEP * value

    for repeat in range(COUPLED):
        speeds = jnp.zeros((points, half), jnp.float32)
        for part in range(parts):
            outer = speed_now[part, :, :, half:width].reshape(count, half)
            picked = jnp.dot(
                pick[...], outer, precision=HIGHEST, preferred_element_type=jnp.float32
            )
            speeds = speeds + normal_cols[part] * picked
        own_speeds[...] = speeds
        packed_out[repeat] = pack(speeds).astype(packed_out.dtype)

        @pl.loop(1, col_count)
        def _(d):
            speed_copy(repeat, d).start()

        packed_in[repeat, col] = packed_out[repeat]

        if repeat == 0:

            @pl.loop(1, row_count)
            def _(d):
                geo_copy(1, d).wait_recv()

            @pl.loop(1, col_count)
            def _(d):
                geo_copy(0, d).wait_recv()

            @pl.loop(0, row_count)
            def _(r):
                for k in range(3):
                    target_cols[r, k] = as_column(targets[r, k : k + 1, :])

            tile(lax.rem(row + 1, row_count))

        @pl.loop(1, col_count)
        def _(d):
            speed_copy(repeat, d).wait_recv()

        @pl.loop(0, parts)
        def _(part):
            send_halos(repeat * SUBSTEPS, part)

        @pl.loop(0, col_count)
        def _(c):
            value = packed_in[repeat, c].astype(jnp.float32)
            unpacked[c, 0 : points // 2, :] = value.astype(jnp.bfloat16)
            unpacked[c, points // 2 : points, :] = pltpu.roll(value, half // 2, 1).astype(
                jnp.bfloat16
            )

        @pl.loop(1, row_count + 1)
        def _(d):
            r = lax.rem(row + d, row_count)
            total = jnp.zeros((points, half), jnp.float32)
            for c in range(col_count):
                total = total + jnp.dot(
                    tiles[r, c], unpacked[c], preferred_element_type=jnp.float32
                )
            partial_out[repeat, r] = pack(total)

            @pl.when(d < row_count)
            def _():
                part_copy(repeat, d).start()
                if repeat == 0:
                    tile(lax.rem(r + 1, row_count))

        received = partial_out[repeat, row]
        for d in range(1, row_count):
            part_copy(repeat, d).wait_recv()
            received = received + partial_in[repeat, d]
        low_points = jnp.concatenate([low_half, low_half], axis=0)
        both = jnp.concatenate([received, pltpu.roll(received, half // 2, 1)], axis=0)
        pressure = jnp.where(low_points, 0.0, 0.5 * own_speeds[...] + both)
        for part in range(parts):
            loading = jnp.dot(
                spread[...], -(normal_cols[part] * pressure),
                precision=HIGHEST, preferred_element_type=jnp.float32,
            )
            load[part] = loading.reshape(breadth, height, half)

            local(part)

        last = (repeat + 1) * SUBSTEPS - 1

        @pl.loop(repeat * SUBSTEPS, last + 1)
        def _(step):
            @pl.loop(0, parts)
            def _(part):
                complete(step, part)

                @pl.when(step < last)
                def _():
                    send_halos(step + 1, part)
                    local(part)

    for part in range(parts):
        for j in range(breadth):
            for lanes in range(2):
                lines = pl.ds(lanes * breadth + j, height, stride=2 * breadth)
                cut = pl.ds(lanes * half, half)
                u_out[part, lines, :] = field[part, REACH + j, middle, cut]
                v_out[part, lines, :] = speed_now[part, j, :, cut]

    @pl.loop(0, COUPLED * SUBSTEPS)
    def _(step):
        for side in range(4):

            @pl.when(present[side])
            def _():
                for part in range(parts):
                    halo_copy(step, side, part, False).wait_send()

    @pl.loop(1, col_count)
    def _(d):
        geo_copy(0, d).wait_send()
        for repeat in range(COUPLED):
            speed_copy(repeat, d).wait_send()

    @pl.loop(1, row_count)
    def _(d):
        geo_copy(1, d).wait_send()
        for repeat in range(COUPLED):
            part_copy(repeat, d).wait_send()


def on_device(shape, displacement, velocity, stiffness, wet_position, wet_normal, wet_area, wet_map):
    col_count, row_count, _ = shape
    parts, height, breadth, width = displacement.shape
    half = width // 2
    points = wet_map.shape[0]
    steps = COUPLED * SUBSTEPS
    stiff = jnp.broadcast_to(stiffness.T[:, :, None], (breadth, height, half))
    node = (wet_map % breadth) * height + wet_map // breadth

    def split(state):
        tiled = state.reshape(parts, height, breadth, 2, half).transpose(0, 1, 3, 2, 4)
        return tiled.reshape(parts, height * 2 * breadth, half)

    def joined(state):
        tiled = state.reshape(parts, height, 2, breadth, half).transpose(0, 1, 3, 2, 4)
        return tiled.reshape(parts, height, breadth, width)

    state = jax.ShapeDtypeStruct((parts, height * 2 * breadth, half), jnp.float32)
    cols = (steps, parts, 2, REACH, height, width)
    rows = (steps, parts, 2, breadth // 2, 8, width)
    f32, bf16 = jnp.float32, jnp.bfloat16
    dma = pltpu.SemaphoreType.DMA
    u_new, v_new = pl.pallas_call(
        functools.partial(coupled_kernel, shape),
        out_shape=(state, state),
        in_specs=[whole_spec()] * 7,
        out_specs=(whole_spec(), whole_spec()),
        scratch_shapes=[
            VMEM((parts, breadth + 2 * REACH, height + 2 * PAD, width), f32),
            VMEM((parts, breadth, height, width), f32),
            VMEM((parts, breadth, height, width), f32),
            VMEM((parts, breadth, height, half), f32),
            VMEM(cols, bf16),
            VMEM(cols, bf16),
            VMEM(rows, f32),
            VMEM(rows, f32),
            VMEM((8, points), f32),
            VMEM((col_count, 8, points), f32),
            VMEM((row_count, 8, points), f32),
            VMEM((row_count, 3, points, half), f32),
            VMEM((parts, points, half), f32),
            VMEM((points, height * breadth), f32),
            VMEM((height * breadth, points), f32),
            VMEM((points, half), f32),
            VMEM((COUPLED, points // 2, half), bf16),
            VMEM((COUPLED, col_count, points // 2, half), bf16),
            VMEM((col_count, points, half), bf16),
            VMEM((row_count, col_count, points, points), bf16),
            VMEM((COUPLED, row_count, points // 2, half), f32),
            VMEM((COUPLED, row_count, points // 2, half), f32),
            dma((steps, parts, 4)),
            dma((steps, parts, 4)),
            dma((2, max(col_count, row_count))),
            dma((2, max(col_count, row_count))),
            dma((COUPLED, col_count)),
            dma((COUPLED, col_count)),
            dma((COUPLED, row_count)),
            dma((COUPLED, row_count)),
        ],
        compiler_params=pltpu.CompilerParams(
            collective_id=0, has_side_effects=True, vmem_limit_bytes=67043328
        ),
        name="coupled_steps",
    )(
        split(displacement), split(velocity), stiff,
        wet_position, wet_normal, wet_area[None, :], node[None, :],
    )
    return (joined(u_new), joined(v_new))


def solution(mesh):
    sizes = mesh.shape
    shape = (sizes["tcol"], sizes["group"] * sizes["trow"], sizes["trow"])
    state = P(None, ("group", "trow"), "tcol", None)
    wet = ("group", "trow", "tcol")
    return jax.shard_map(
        functools.partial(on_device, shape),
        mesh=mesh,
        in_specs=(
            state,
            state,
            P(("group", "trow"), "tcol"),
            P(None, wet),
            P(None, wet),
            P(wet),
            P(wet),
        ),
        out_specs=(state, state),
        check_vma=False,
    )
```
